256 devices in a mesh: mode: 4 (over x), rest: 64 (over y, z, core).
Axes of the slice: x: 4, y: 4, z: 8, core: 2. Of those that a mesh axis runs over, the one named last changes fastest.
Arguments:
- unfolded: float32 [512, 524288], P('mode', 'rest'), may hold values from -150 to 150
- start_block: float32 [512, 128], replicated, may hold values from -6 to 6
Outputs:
- triangle: float32 [512, 512], replicated
- factor: float32 [512, 128], replicated
- core: float32 [128, 524288], P('mode', 'rest')
The draws below stay inside these ranges and needn't reach their ends.
All inputs are finite; a program needn't handle non-finite values.
Results may differ from the reference program's by a relative error of at most 0.0003.
Values sent between devices are 32-bit elements; how exact they have to be, the bound alone decides.
No kernel may reach another device: no remote copies, remote signals or barrier semaphores. Data moves between devices by JAX's collectives and lax.ppermute only.
A program may use at most 64 MiB of HBM per device.

```python
import math
import jax
import jax.numpy as jnp
from jax import lax

M = 512
R = 128
ITERS = 3
COLS = 524288


def draw_unfolded(key, part):
    keys = jax.random.split(jax.random.fold_in(key, 11), 4)
    noise = jax.random.truncated_normal(keys[0], -5.0, 5.0, (M, COLS), jnp.float32)
    col_low = math.log(0.7)
    col_high = math.log(1.4)
    mixing = jnp.eye(M, dtype=jnp.float32) + 0.03 * jax.random.normal(keys[1], (M, M), jnp.float32)
    row_scale = jnp.exp(jax.random.uniform(keys[2], (M,), jnp.float32, 0.0, math.log(4.0)))
    position = jnp.arange(COLS, dtype=jnp.float32) / COLS
    col_scale = (1.0 + 2.0 * position) * jnp.exp(jax.random.uniform(keys[3], (COLS,), jnp.float32, col_low, col_high))
    mixed = jnp.dot(mixing, noise, precision=lax.Precision.HIGHEST)
    return row_scale[:, None] * mixed * col_scale[None, :]


def gaussian(stream_key, extent, width, reach, kind=jnp.bfloat16):
    values = width * jax.random.normal(stream_key, extent, jnp.float32)
    return jnp.clip(values, min=-reach, max=reach).astype(kind)


def setup_inputs(seed: int = 0) -> dict:
    key_list = jax.random.split(jax.random.key(seed), 3)
    unfolded = draw_unfolded(jax.random.fold_in(key_list[2], 71), 0)
    start_block = gaussian(key_list[1], (M, R), 1.0, 6.0, jnp.float32)
    return dict(unfolded=unfolded, start_block=start_block)


def orthogonal_steps(triangle, start_block):
    highest = lax.Precision.HIGHEST
    columns_now = start_block
    for repeat in range(ITERS):
        inner = jnp.dot(triangle.T, columns_now, precision=highest)
        image = jnp.dot(triangle, inner, precision=highest)
        projected = jnp.dot(image.T, image, precision=highest)
        small_factor = jnp.linalg.cholesky(projected)
        columns_now = lax.linalg.triangular_solve(small_factor, image, left_side=False, lower=True, transpose_a=True)
    return columns_now

def reference(unfolded, start_block):
    highest = lax.Precision.HIGHEST
    gram = jnp.dot(unfolded, unfolded.T, precision=highest) / COLS
    triangle = jnp.linalg.cholesky(gram)
    factor = orthogonal_steps(triangle, start_block)
    core = jnp.dot(factor.T, unfolded, precision=highest)
    return (triangle, factor, core)
```

```python
import functools

import jax
import jax.numpy as jnp
from jax import lax
from jax.experimental import pallas as pl
from jax.experimental.pallas import tpu as pltpu
from jax.sharding import Mesh, PartitionSpec as P

ITERS = 3
HIGHEST = lax.Precision.HIGHEST
NB = 128
NT = (((1,), (1,)), ((), ()))
TN = (((0,), (0,)), ((), ()))
F32 = jnp.float32


def dot_exact(a, b, dims=(((1,), (0,)), ((), ()))):
    return lax.dot_general(a, b, dims, precision=HIGHEST, preferred_element_type=F32)


def cholesky_block(matrix, inverse_ref, upper_ref=None):
    n = matrix.shape[0]
    shape = (8, n)
    spread = functools.partial(jnp.broadcast_to, shape=shape)
    lane = lax.broadcasted_iota(jnp.int32, shape, 1)
    sub = lax.broadcasted_iota(jnp.int32, shape, 0)
    rows = [matrix[8 * i : 8 * i + 8, :] for i in range(n // 8)]
    for t in range(n // 8):
        first = 8 * t
        inside = (lane >= first) & (lane < first + 8)
        cols = {
            i: [spread(rows[i][:, first + j : first + j + 1]) for j in range(8)]
            for i in range(t, n // 8)
        }
        own = cols[t]
        top = rows[t]
        unit = jnp.where(lane == first + sub, 1.0, 0.0)
        recips = []
        mults = {i: [] for i in range(t + 1, n // 8)}
        for j in range(8):
            recip = 1.0 / spread(own[j][j : j + 1, :])
            recips.append(recip)
            mult = jnp.where(sub > j, own[j] * recip, 0.0)
            top = top - mult * spread(top[j : j + 1, :])
            unit = unit - mult * spread(unit[j : j + 1, :])
            pivot_row = {l: spread(own[l][j : j + 1, :]) for l in range(j + 1, 8)}
            for i in range(t + 1, n // 8):
                mult = cols[i][j] * recip
                mults[i].append(mult)
                for l in range(j + 1, 8):
                    cols[i][l] = cols[i][l] - mult * pivot_row[l]
            for l in range(j + 1, 8):
                own[l] = own[l] - (own[j] * pivot_row[l]) * recip
        scale = recips[0]
        for j in range(1, 8):
            scale = jnp.where(sub == j, recips[j], scale)
        scale = lax.rsqrt(1.0 / scale)
        inverse_ref[first : first + 8, :] = scale * jnp.where(lane < first, top, unit)
        if upper_ref is not None:
            upper_ref[first : first + 8, :] = jnp.where(lane >= first + sub, scale * top, 0.0)
        source = jnp.where(inside, unit, top)
        for i in range(t + 1, n // 8):
            left = jnp.where(inside, 0.0, rows[i])
            for j in range(8):
                left = left - mults[i][j] * spread(source[j : j + 1, :])
            rows[i] = left


def block_index(i, j):
    return i * (i + 1) // 2 + j


def gram_kernel(x_ref, out_ref, acc_ref):
    step = pl.program_id(0)
    m = x_ref.shape[0]
    half = m // 2
    x = x_ref[...]
    high = x.astype(jnp.bfloat16)
    low = (x - high.astype(F32)).astype(jnp.bfloat16)

    def product(r, c):
        dot = functools.partial(lax.dot_general, dimension_numbers=NT, preferred_element_type=F32)
        small = dot(low[r], low[c]) + (dot(high[r], low[c]) + dot(low[r], high[c]))
        return dot(high[r], high[c]) + small

    upper, lower, whole = slice(0, half), slice(half, m), slice(0, m)

    @pl.when(step == 0)
    def _():
        acc_ref[upper, upper] = product(upper, upper)
        acc_ref[lower, whole] = product(lower, whole)

    @pl.when(step > 0)
    def _():
        acc_ref[upper, upper] += product(upper, upper)
        acc_ref[lower, whole] += product(lower, whole)

    @pl.when(step == pl.num_programs(0) - 1)
    def _():
        for i in range(m // NB):
            for j in range(i + 1):
                b = block_index(i, j)
                out_ref[b * NB : (b + 1) * NB, :] = acc_ref[i * NB : (i + 1) * NB, j * NB : (j + 1) * NB]


def gram_lower(full_rows):
    m, cols = full_rows.shape
    nblk = m // NB
    rows_out = nblk * (nblk + 1) // 2 * NB
    tile = min(512, cols)
    return pl.pallas_call(
        gram_kernel,
        grid=(cols // tile,),
        in_specs=[pl.BlockSpec((m, tile), lambda k: (0, k))],
        out_specs=pl.BlockSpec((rows_out, NB), lambda k: (0, 0)),
        out_shape=jax.ShapeDtypeStruct((rows_out, NB), F32),
        scratch_shapes=[pltpu.VMEM((m, m), F32)],
        compiler_params=pltpu.CompilerParams(vmem_limit_bytes=48 << 20),
        name="gram_lower",
    )(full_rows)


def factor_kernel(scale, core_ref, gram_ref, start_ref, tri_ref, basis_ref, full_ref, inv_ref, up_ref):
    m = tri_ref.shape[0]
    nblk = m // NB

    def sl(i):
        return slice(i * NB, (i + 1) * NB)

    def block(i, j):
        return gram_ref[sl(block_index(i, j)), :] * scale

    @pl.when(core_ref[0] == 0)
    def _():
        for i in range(nblk):
            for j in range(i + 1):
                full_ref[sl(i), sl(j)] = block(i, j)
        for p in range(nblk):
            cholesky_block(full_ref[sl(p), sl(p)], inv_ref, up_ref)
            tri_ref[sl(p), sl(p)] = up_ref[...].T
            for i in range(p):
                tri_ref[sl(i), sl(p)] = jnp.zeros((NB, NB), F32)
            if p + 1 < nblk:
                below = dot_exact(full_ref[(p + 1) * NB :, sl(p)], inv_ref[...], NT)
                tri_ref[(p + 1) * NB :, sl(p)] = below
                for j in range(p + 1, nblk):
                    lo = (j - p - 1) * NB
                    full_ref[j * NB :, sl(j)] -= dot_exact(below[lo:, :], below[lo : lo + NB, :], NT)

    @pl.when(core_ref[0] != 0)
    def _():
        for i in range(nblk):
            for j in range(i + 1):
                b = block(i, j)
                full_ref[sl(i), sl(j)] = b
                if j < i:
                    full_ref[sl(j), sl(i)] = b.T
        basis_ref[...] = start_ref[...]

        def step(_, carry):
            image = dot_exact(full_ref[...], basis_ref[...])
            cholesky_block(dot_exact(image, image, TN), inv_ref)
            basis_ref[...] = dot_exact(image, inv_ref[...], NT)
            return carry

        lax.fori_loop(0, ITERS, step, 0)


def factorize(core, gram, start_block, scale):
    m, r = start_block.shape
    vmem = pl.BlockSpec(memory_space=pltpu.VMEM)
    return pl.pallas_call(
        functools.partial(factor_kernel, scale),
        in_specs=[pl.BlockSpec(memory_space=pltpu.SMEM), vmem, vmem],
        out_specs=[vmem, vmem],
        out_shape=[jax.ShapeDtypeStruct((m, m), F32), jax.ShapeDtypeStruct((m, r), F32)],
        scratch_shapes=[pltpu.VMEM((m, m), F32), pltpu.VMEM((NB, NB), F32), pltpu.VMEM((NB, NB), F32)],
        compiler_params=pltpu.CompilerParams(vmem_limit_bytes=48 << 20),
        name="factorize",
    )(core.reshape(1).astype(jnp.int32), gram, start_block)


def swap_cores(value):
    return lax.ppermute(value, "core", [(0, 1), (1, 0)])


def spread_out(value, axes):
    n = lax.axis_size(axes)
    copies = jnp.broadcast_to(value[None], (n,) + value.shape)
    return lax.all_to_all(copies, axes, 0, 0, tiled=True)


def sum_everywhere(part):
    core = lax.axis_index("core")
    rows, lanes = part.shape
    halves = part.reshape(2, rows // 2, lanes)
    mine = lax.dynamic_index_in_dim(halves, core, 0, keepdims=False)
    other = lax.dynamic_index_in_dim(halves, 1 - core, 0, keepdims=False)
    mine = mine + swap_cores(other)
    plane = ("mode", "y")
    n = lax.axis_size(plane)
    pieces = lax.all_to_all(mine.reshape(n, rows // 2 // n, lanes), plane, 0, 0, tiled=True)
    piece = spread_out(pieces.sum(0), "z").sum(0)
    mine = spread_out(piece, plane).reshape(rows // 2, lanes)
    other = swap_cores(mine)
    first = core == 0
    return jnp.concatenate([jnp.where(first, mine, other), jnp.where(first, other, mine)], axis=0)


def per_device(unfolded, start_block):
    total_cols = unfolded.shape[1] * lax.axis_size(("y", "z", "core"))
    full_rows = lax.all_to_all(unfolded, "mode", split_axis=1, concat_axis=0, tiled=True)
    gram = sum_everywhere(gram_lower(full_rows))
    core_id = lax.axis_index("core")
    tri, basis = factorize(core_id, gram, start_block, 1.0 / total_cols)
    factor = jnp.where(core_id == 1, basis, swap_cores(basis))
    triangle = jnp.where(core_id == 0, tri, swap_cores(tri))
    partial_value = jnp.dot(factor.T, full_rows, precision=HIGHEST)
    core = lax.all_to_all(partial_value, "mode", split_axis=0, concat_axis=1, tiled=True)
    return (triangle, factor, core)


def solution(mesh):
    fine = Mesh(mesh.devices.reshape(4, 4, 8, 2), ("mode", "y", "z", "core"))
    rest = ("y", "z", "core")
    return jax.shard_map(
        per_device,
        mesh=fine,
        in_specs=(P("mode", rest), P()),
        out_specs=(P(), P(), P("mode", rest)),
        check_vma=False,
    )
```

```python
import functools

import jax
import jax.numpy as jnp
from jax import lax
from jax.experimental import pallas as pl
from jax.experimental.pallas import tpu as pltpu
from jax.sharding import Mesh, PartitionSpec as P

ITERS = 3
MODE = 4
WIDTHS = (1024, 1024)
TILE = 512
HIGHEST = lax.Precision.HIGHEST
NB = 128
NT = (((1,), (1,)), ((), ()))
TN = (((0,), (0,)), ((), ()))
F32 = jnp.float32


def dot_exact(a, b, dims=(((1,), (0,)), ((), ()))):
    return lax.dot_general(a, b, dims, precision=HIGHEST, preferred_element_type=F32)


def cholesky_block(matrix, inverse_ref, upper_ref=None):
    n = matrix.shape[0]
    shape = (8, n)
    spread = functools.partial(jnp.broadcast_to, shape=shape)
    lane = lax.broadcasted_iota(jnp.int32, shape, 1)
    sub = lax.broadcasted_iota(jnp.int32, shape, 0)
    rows = [matrix[8 * i : 8 * i + 8, :] for i in range(n // 8)]
    for t in range(n // 8):
        first = 8 * t
        inside = (lane >= first) & (lane < first + 8)
        cols = {
            i: [spread(rows[i][:, first + j : first + j + 1]) for j in range(8)]
            for i in range(t, n // 8)
        }
        own = cols[t]
        top = rows[t]
        unit = jnp.where(lane == first + sub, 1.0, 0.0)
        recips = []
        mults = {i: [] for i in range(t + 1, n // 8)}
        for j in range(8):
            recip = 1.0 / spread(own[j][j : j + 1, :])
            recips.append(recip)
            mult = jnp.where(sub > j, own[j] * recip, 0.0)
            top = top - mult * spread(top[j : j + 1, :])
            unit = unit - mult * spread(unit[j : j + 1, :])
            pivot_row = {l: spread(own[l][j : j + 1, :]) for l in range(j + 1, 8)}
            for i in range(t + 1, n // 8):
                mult = cols[i][j] * recip
                mults[i].append(mult)
                for l in range(j + 1, 8):
                    cols[i][l] = cols[i][l] - mult * pivot_row[l]
            for l in range(j + 1, 8):
                own[l] = own[l] - (own[j] * pivot_row[l]) * recip
        scale = recips[0]
        for j in range(1, 8):
            scale = jnp.where(sub == j, recips[j], scale)
        scale = lax.rsqrt(1.0 / scale)
        inverse_ref[first : first + 8, :] = scale * jnp.where(lane < first, top, unit)
        if upper_ref is not None:
            upper_ref[first : first + 8, :] = jnp.where(lane >= first + sub, scale * top, 0.0)
        source = jnp.where(inside, unit, top)
        for i in range(t + 1, n // 8):
            left = jnp.where(inside, 0.0, rows[i])
            for j in range(8):
                left = left - mults[i][j] * spread(source[j : j + 1, :])
            rows[i] = left


def block_index(i, j):
    return i * (i + 1) // 2 + j


VMEM = pl.BlockSpec(memory_space=pltpu.VMEM)
SMEM = pl.BlockSpec(memory_space=pltpu.SMEM)
BF16 = jnp.bfloat16


def limit(mib):
    return pltpu.CompilerParams(vmem_limit_bytes=mib << 20)


def high_low(value):
    high = value.astype(BF16)
    return high, (value - high.astype(F32)).astype(BF16)


def gram_kernel(has_prior, final, place_ref, *refs):
    pieces, refs = refs[:MODE], refs[MODE:]
    prior_ref, refs = (refs[0], refs[1:]) if has_prior else (None, refs)
    wide_ref, outs, acc_ref = refs[0], refs[1:-1], refs[-1]
    m = acc_ref.shape[0]
    half = m // 2
    cols = pieces[0].shape[1]
    upper, lower, whole = slice(0, half), slice(half, m), slice(0, m)
    dot = functools.partial(lax.dot_general, dimension_numbers=NT, preferred_element_type=F32)
    for t in range(cols // TILE):
        for k, piece in enumerate(pieces):
            rows = pl.ds(pl.multiple_of(((place_ref[0] - k) & (MODE - 1)) * NB, NB), NB)
            high, low = high_low(piece[:, t * TILE : (t + 1) * TILE])
            wide_ref[rows, 2 * t * TILE : (2 * t + 1) * TILE] = high
            wide_ref[rows, (2 * t + 1) * TILE : (2 * t + 2) * TILE] = low

        def product(r, c):
            left = wide_ref[r, 2 * t * TILE : (2 * t + 2) * TILE]
            high = wide_ref[c, 2 * t * TILE : (2 * t + 1) * TILE]
            low = wide_ref[c, (2 * t + 1) * TILE : (2 * t + 2) * TILE]
            straight, turned = jnp.concatenate([high, low], axis=1), jnp.concatenate([low, high], axis=1)
            return dot(left, straight) + dot(left, turned)

        if t == 0:
            acc_ref[upper, upper] = product(upper, upper)
            acc_ref[lower, whole] = product(lower, whole)
        else:
            acc_ref[upper, upper] += product(upper, upper)
            acc_ref[lower, whole] += product(lower, whole)

    share = outs[0].shape[0] // NB

    def write(first, second):
        for i in range(m // NB):
            for j in range(i + 1):
                b = block_index(i, j)
                value = acc_ref[i * NB : (i + 1) * NB, j * NB : (j + 1) * NB]
                if prior_ref is not None:
                    value = value + prior_ref[b * NB : (b + 1) * NB, :]
                target = first if b < share else second
                target[b % share * NB : (b % share + 1) * NB, :] = value

    if final:
        pl.when(place_ref[1] == 0)(lambda: write(outs[0], outs[1]))
        pl.when(place_ref[1] != 0)(lambda: write(outs[1], outs[0]))
    else:
        write(outs[0], None)


def gram_lower(place, pieces, prior, final):
    rows, cols = pieces[0].shape
    m = rows * MODE
    rows_out = MODE * (MODE + 1) // 2 * NB
    priors = [] if prior is None else [prior]
    heights = [rows_out // 2] * 2 if final else [rows_out]
    return pl.pallas_call(
        functools.partial(gram_kernel, prior is not None, final),
        in_specs=[SMEM] + [VMEM] * (MODE + len(priors)),
        out_specs=[VMEM] * (1 + len(heights)),
        out_shape=[jax.ShapeDtypeStruct((m, 2 * cols), BF16)] + [jax.ShapeDtypeStruct((h, NB), F32) for h in heights],
        scratch_shapes=[pltpu.VMEM((m, m), F32)],
        compiler_params=limit(20),
        name="gram_lower",
    )(place, *pieces, *priors)


def core_kernel(place_ref, mine_ref, other_ref, wide_ref, *refs):
    outs, (result_ref, turned_ref) = refs[:MODE], refs[MODE:]
    r = mine_ref.shape[1]
    factor = jnp.where(place_ref[1] == 1, mine_ref[...], other_ref[...])
    turned_ref[:r, :], turned_ref[r:, :] = high_low(factor.T)
    for t in range(wide_ref.shape[1] // (2 * TILE)):
        both = jnp.dot(turned_ref[...], wide_ref[:, 2 * t * TILE : (2 * t + 2) * TILE], preferred_element_type=F32)
        big, small = both[:, :TILE], both[:, TILE:]
        result_ref[:, t * TILE : (t + 1) * TILE] = big[:r, :] + (big[r:, :] + (small[:r, :] + small[r:, :]))
    share = outs[0].shape[0]
    for k, out in enumerate(outs):
        at = pl.multiple_of(((place_ref[0] + k) & (MODE - 1)) * share, share)
        out[...] = result_ref[pl.ds(at, share), :]


def core_rows(place, mine, other, wide):
    m, r = mine.shape
    cols = wide.shape[1] // 2
    return pl.pallas_call(
        core_kernel,
        in_specs=[SMEM] + [VMEM] * 3,
        out_specs=[VMEM] * MODE,
        out_shape=[jax.ShapeDtypeStruct((r // MODE, cols), F32)] * MODE,
        scratch_shapes=[pltpu.VMEM((r, cols), F32), pltpu.VMEM((2 * r, m), BF16)],
        compiler_params=limit(16),
        name="core_rows",
    )(place, mine, other, wide)


def factor_kernel(scale, place_ref, mine_ref, other_ref, start_ref, tri_ref, basis_ref, full_ref, inv_ref, up_ref):
    m = full_ref.shape[0]
    nblk = m // NB

    def sl(i):
        return slice(i * NB, (i + 1) * NB)

    share = mine_ref.shape[0] // NB

    def block(halves, i, j):
        b = block_index(i, j)
        return halves[b // share][sl(b % share), :] * scale

    @pl.when(place_ref[1] == 0)
    def _():
        for i in range(nblk):
            for j in range(i + 1):
                full_ref[sl(i), sl(j)] = block((mine_ref, other_ref), i, j)

        def panel(p, carry):
            here = pl.ds(pl.multiple_of(p * NB, NB), NB)
            cholesky_block(full_ref[here, here], inv_ref, up_ref)
            column = dot_exact(full_ref[:, here], inv_ref[...], NT)
            row = lax.broadcasted_iota(jnp.int32, column.shape, 0)
            below = jnp.where(row >= (p + 1) * NB, column, 0.0)
            full_ref[:, here] = below

            @pl.when(p + 1 < nblk)
            def _():
                for j in range(1, nblk):
                    @pl.when(p < j)
                    def _():
                        full_ref[j * NB :, sl(j)] -= dot_exact(below[j * NB :, :], below[sl(j), :], NT)

            full_ref[here, here] = up_ref[...].T
            return carry

        lax.fori_loop(0, nblk, panel, 0)
        for i in range(nblk):
            for j in range(i + 1):
                tri_ref[sl(block_index(i, j)), :] = full_ref[sl(i), sl(j)]

    @pl.when(place_ref[1] != 0)
    def _():
        for i in range(nblk):
            for j in range(i + 1):
                b = block((other_ref, mine_ref), i, j)
                full_ref[sl(i), sl(j)] = b
                if j < i:
                    full_ref[sl(j), sl(i)] = b.T
        basis_ref[...] = start_ref[...]

        def step(_, carry):
            image = dot_exact(full_ref[...], basis_ref[...])
            cholesky_block(dot_exact(image, image, TN), inv_ref)
            basis_ref[...] = dot_exact(image, inv_ref[...], NT)
            return carry

        lax.fori_loop(0, ITERS, step, 0)


def factorize(place, mine, other, start_block, scale):
    m, r = start_block.shape
    packed = (2 * mine.shape[0], NB)
    return pl.pallas_call(
        functools.partial(factor_kernel, scale),
        in_specs=[SMEM, VMEM, VMEM, VMEM],
        out_specs=[VMEM, VMEM],
        out_shape=[jax.ShapeDtypeStruct(packed, F32), jax.ShapeDtypeStruct((m, r), F32)],
        scratch_shapes=[pltpu.VMEM((m, m), F32), pltpu.VMEM((NB, NB), F32), pltpu.VMEM((NB, NB), F32)],
        compiler_params=limit(24),
        name="factorize",
    )(place, mine, other, start_block)


def unpack_kernel(place_ref, mine_ref, other_ref, tri_ref):
    nblk = tri_ref.shape[0] // NB

    def fill(source):
        for i in range(nblk):
            for j in range(nblk):
                b = block_index(i, j)
                value = source[b * NB : (b + 1) * NB, :] if j <= i else jnp.zeros((NB, NB), F32)
                tri_ref[i * NB : (i + 1) * NB, j * NB : (j + 1) * NB] = value

    pl.when(place_ref[1] == 0)(lambda: fill(mine_ref))
    pl.when(place_ref[1] != 0)(lambda: fill(other_ref))


def unpack_triangle(place, mine, other):
    m = MODE * NB
    return pl.pallas_call(
        unpack_kernel,
        in_specs=[SMEM, VMEM, VMEM],
        out_specs=VMEM,
        out_shape=jax.ShapeDtypeStruct((m, m), F32),
        compiler_params=limit(16),
        name="unpack_triangle",
    )(place, mine, other)


def swap_cores(value):
    return lax.ppermute(value, "core", [(0, 1), (1, 0)])


def shift(value, axis, by):
    n = lax.axis_size(axis)
    return lax.ppermute(value, axis, [(i, (i + by) % n) for i in range(n)])


def spread_out(value, axes):
    n = lax.axis_size(axes)
    copies = jnp.broadcast_to(value[None], (n,) + value.shape)
    return lax.all_to_all(copies, axes, 0, 0, tiled=True)


def sum_z(value):
    value = value + lax.ppermute(value, "z", [(i, i ^ 1) for i in range(8)])
    side, back, other = (shift(value, "z", 2), shift(value, "z", 6), shift(value, "z", 4))
    return (value + other) + (side + back)


def sum_everywhere(mine, other):
    rows, lanes = mine.shape
    mine = mine + swap_cores(other)
    plane = ("mode", "y")
    n = lax.axis_size(plane)
    pieces = lax.all_to_all(mine.reshape(n, rows // n, lanes), plane, 0, 0, tiled=True)
    piece = sum_z(pieces.sum(0))
    mine = spread_out(piece, plane).reshape(rows, lanes)
    return mine, swap_cores(mine)


def per_device(unfolded, start_block):
    total_cols = unfolded.shape[1] * lax.axis_size(("y", "z", "core"))
    position, core_id = lax.axis_index("mode"), lax.axis_index("core")
    place = jnp.stack([position, core_id]).astype(jnp.int32)
    share = unfolded.shape[1] // MODE
    starts = [sum(WIDTHS[:c]) for c in range(len(WIDTHS))]

    def columns(source, k, c):
        owner = (position + k) & (MODE - 1)
        return lax.dynamic_slice_in_dim(source, owner * share + starts[c], WIDTHS[c], axis=1)

    received, source = [], unfolded
    for c in range(len(WIDTHS)):
        sent = {k: columns(source, k, c) for k in (2, 1, 3)}
        source, _ = lax.optimization_barrier((source, sent[2]))
        received.append([shift(sent[k], "mode", k) for k in range(1, MODE)])
    own = [columns(source, 0, c) for c in range(len(WIDTHS))]
    sums, wides = [None], []
    for c in range(len(WIDTHS)):
        wide, *sums = gram_lower(place, [own[c]] + received[c], sums[0], c == len(WIDTHS) - 1)
        wides.append(wide)
    sums = sum_everywhere(*sums)
    tri, basis = factorize(place, *sums, start_block, 1.0 / total_cols)
    basis_there = swap_cores(basis)
    factor = jnp.where(core_id == 1, basis, basis_there)
    triangle = unpack_triangle(place, tri, swap_cores(tri))
    landed = []
    for c, wide in enumerate(wides):
        parts = core_rows(place, basis, basis_there, wide)
        for k in (2, 1, 3, 0):
            got = shift(parts[k], "mode", k) if k else parts[0]
            landed.append((((position - k) & (MODE - 1)) * share + starts[c], got))
    core = jnp.zeros((factor.shape[1] // MODE, MODE * share), F32)
    core, triangle, factor, _ = lax.optimization_barrier((core, triangle, factor, parts[0]))
    for at, got in landed:
        core = lax.dynamic_update_slice_in_dim(core, got, at, axis=1)
    return (triangle, factor, core)


def solution(mesh):
    fine = Mesh(mesh.devices.reshape(4, 4, 8, 2), ("mode", "y", "z", "core"))
    rest = ("y", "z", "core")
    return jax.shard_map(
        per_device,
        mesh=fine,
        in_specs=(P("mode", rest), P()),
        out_specs=(P(), P(), P("mode", rest)),
        check_vma=False,
    )
```

```python
import functools

import jax
import jax.numpy as jnp
from jax import lax
from jax.experimental import pallas as pl
from jax.experimental.pallas import tpu as pltpu
from jax.sharding import Mesh, PartitionSpec as P

ITERS = 3
MODE = 4
WIDTHS = (1024, 1024)
TILE = 512
HIGHEST = lax.Precision.HIGHEST
NB = 128
NT = (((1,), (1,)), ((), ()))
TN = (((0,), (0,)), ((), ()))
F32 = jnp.float32


def dot_exact(a, b, dims=(((1,), (0,)), ((), ()))):
    return lax.dot_general(a, b, dims, precision=HIGHEST, preferred_element_type=F32)


def cholesky_block(matrix, inverse_ref, upper_ref=None):
    n = matrix.shape[0]
    shape = (8, n)
    spread = functools.partial(jnp.broadcast_to, shape=shape)
    lane = lax.broadcasted_iota(jnp.int32, shape, 1)
    sub = lax.broadcasted_iota(jnp.int32, shape, 0)
    rows = [matrix[8 * i : 8 * i + 8, :] for i in range(n // 8)]
    for t in range(n // 8):
        first = 8 * t
        inside = (lane >= first) & (lane < first + 8)
        cols = {
            i: [spread(rows[i][:, first + j : first + j + 1]) for j in range(8)]
            for i in range(t, n // 8)
        }
        own = cols[t]
        top = rows[t]
        unit = jnp.where(lane == first + sub, 1.0, 0.0)
        recips = []
        mults = {i: [] for i in range(t + 1, n // 8)}
        for j in range(8):
            recip = 1.0 / spread(own[j][j : j + 1, :])
            recips.append(recip)
            mult = jnp.where(sub > j, own[j] * recip, 0.0)
            top = top - mult * spread(top[j : j + 1, :])
            unit = unit - mult * spread(unit[j : j + 1, :])
            pivot_row = {l: spread(own[l][j : j + 1, :]) for l in range(j + 1, 8)}
            for i in range(t + 1, n // 8):
                mult = cols[i][j] * recip
                mults[i].append(mult)
                for l in range(j + 1, 8):
                    cols[i][l] = cols[i][l] - mult * pivot_row[l]
            for l in range(j + 1, 8):
                own[l] = own[l] - (own[j] * pivot_row[l]) * recip
        scale = recips[0]
        for j in range(1, 8):
            scale = jnp.where(sub == j, recips[j], scale)
        scale = lax.rsqrt(1.0 / scale)
        inverse_ref[first : first + 8, :] = scale * jnp.where(lane < first, top, unit)
        if upper_ref is not None:
            upper_ref[first : first + 8, :] = jnp.where(lane >= first + sub, scale * top, 0.0)
        source = jnp.where(inside, unit, top)
        for i in range(t + 1, n // 8):
            left = jnp.where(inside, 0.0, rows[i])
            for j in range(8):
                left = left - mults[i][j] * spread(source[j : j + 1, :])
            rows[i] = left


def block_index(i, j):
    return i * (i + 1) // 2 + j


VMEM = pl.BlockSpec(memory_space=pltpu.VMEM)
SMEM = pl.BlockSpec(memory_space=pltpu.SMEM)
BF16 = jnp.bfloat16
NO_COST = pl.CostEstimate(flops=0, transcendentals=0, bytes_accessed=0)


def limit(mib):
    return pltpu.CompilerParams(vmem_limit_bytes=mib << 20)


def high_low(value):
    high = value.astype(BF16)
    return high, (value - high.astype(F32)).astype(BF16)


def slice_kernel(shifts, start, share, place_ref, source_ref, *refs):
    outs, sem = refs[:-1], refs[-1]
    width = outs[0].shape[1]
    copies = []
    for n, k in enumerate(shifts):
        at = pl.multiple_of(((place_ref[0] + k) & (MODE - 1)) * share + start, NB)
        copies.append(pltpu.make_async_copy(source_ref.at[:, pl.ds(at, width)], outs[n], sem.at[n]))
        copies[-1].start()
    for copy in copies:
        copy.wait()


def column_slices(place, source, shifts, start, width):
    rows, cols = source.shape
    return pl.pallas_call(
        functools.partial(slice_kernel, shifts, start, cols // MODE),
        in_specs=[SMEM, pl.BlockSpec(memory_space=pl.ANY)],
        out_specs=[VMEM] * len(shifts),
        out_shape=[jax.ShapeDtypeStruct((rows, width), F32)] * len(shifts),
        scratch_shapes=[pltpu.SemaphoreType.DMA((len(shifts),))],
        compiler_params=limit(4),
        cost_estimate=NO_COST,
        name="column_slices",
    )(place, source)


def gram_kernel(has_prior, final, place_ref, *refs):
    pieces, refs = refs[:MODE], refs[MODE:]
    prior_ref, refs = (refs[0], refs[1:]) if has_prior else (None, refs)
    wide_ref, outs, acc_ref = refs[0], refs[1:-1], refs[-1]
    m = acc_ref.shape[0]
    half = m // 2
    cols = pieces[0].shape[1]
    upper, lower, whole = slice(0, half), slice(half, m), slice(0, m)
    dot = functools.partial(lax.dot_general, dimension_numbers=NT, preferred_element_type=F32)
    for t in range(cols // TILE):
        for k, piece in enumerate(pieces):
            rows = pl.ds(pl.multiple_of(((place_ref[0] - k) & (MODE - 1)) * NB, NB), NB)
            high, low = high_low(piece[:, t * TILE : (t + 1) * TILE])
            wide_ref[rows, 2 * t * TILE : (2 * t + 1) * TILE] = high
            wide_ref[rows, (2 * t + 1) * TILE : (2 * t + 2) * TILE] = low

        def product(r, c):
            left = wide_ref[r, 2 * t * TILE : (2 * t + 2) * TILE]
            high = wide_ref[c, 2 * t * TILE : (2 * t + 1) * TILE]
            low = wide_ref[c, (2 * t + 1) * TILE : (2 * t + 2) * TILE]
            straight, turned = jnp.concatenate([high, low], axis=1), jnp.concatenate([low, high], axis=1)
            return dot(left, straight) + dot(left, turned)

        if t == 0:
            acc_ref[upper, upper] = product(upper, upper)
            acc_ref[lower, whole] = product(lower, whole)
        else:
            acc_ref[upper, upper] += product(upper, upper)
            acc_ref[lower, whole] += product(lower, whole)

    share = outs[0].shape[0] // NB

    def write(first, second):
        for i in range(m // NB):
            for j in range(i + 1):
                b = block_index(i, j)
                value = acc_ref[i * NB : (i + 1) * NB, j * NB : (j + 1) * NB]
                if prior_ref is not None:
                    value = value + prior_ref[b * NB : (b + 1) * NB, :]
                target = first if b < share else second
                target[b % share * NB : (b % share + 1) * NB, :] = value

    if final:
        pl.when(place_ref[1] == 0)(lambda: write(outs[0], outs[1]))
        pl.when(place_ref[1] != 0)(lambda: write(outs[1], outs[0]))
    else:
        write(outs[0], None)


def gram_lower(place, pieces, prior, final):
    rows, cols = pieces[0].shape
    m = rows * MODE
    rows_out = MODE * (MODE + 1) // 2 * NB
    priors = [] if prior is None else [prior]
    heights = [rows_out // 2] * 2 if final else [rows_out]
    return pl.pallas_call(
        functools.partial(gram_kernel, prior is not None, final),
        in_specs=[SMEM] + [VMEM] * (MODE + len(priors)),
        out_specs=[VMEM] * (1 + len(heights)),
        out_shape=[jax.ShapeDtypeStruct((m, 2 * cols), BF16)] + [jax.ShapeDtypeStruct((h, NB), F32) for h in heights],
        scratch_shapes=[pltpu.VMEM((m, m), F32)],
        compiler_params=limit(8),
        cost_estimate=NO_COST,
        name="gram_lower",
    )(place, *pieces, *priors)


def core_kernel(place_ref, mine_ref, other_ref, wide_ref, *refs):
    outs, (result_ref, turned_ref) = refs[:MODE], refs[MODE:]
    r = mine_ref.shape[1]
    factor = jnp.where(place_ref[1] == 1, mine_ref[...], other_ref[...])
    turned_ref[:r, :], turned_ref[r:, :] = high_low(factor.T)
    for t in range(wide_ref.shape[1] // (2 * TILE)):
        both = jnp.dot(turned_ref[...], wide_ref[:, 2 * t * TILE : (2 * t + 2) * TILE], preferred_element_type=F32)
        big, small = both[:, :TILE], both[:, TILE:]
        result_ref[:, t * TILE : (t + 1) * TILE] = big[:r, :] + (big[r:, :] + (small[:r, :] + small[r:, :]))
    share = outs[0].shape[0]
    for k, out in enumerate(outs):
        at = pl.multiple_of(((place_ref[0] + k) & (MODE - 1)) * share, share)
        out[...] = result_ref[pl.ds(at, share), :]


def core_rows(place, mine, other, wide):
    m, r = mine.shape
    cols = wide.shape[1] // 2
    return pl.pallas_call(
        core_kernel,
        in_specs=[SMEM] + [VMEM] * 3,
        out_specs=[VMEM] * MODE,
        out_shape=[jax.ShapeDtypeStruct((r // MODE, cols), F32)] * MODE,
        scratch_shapes=[pltpu.VMEM((r, cols), F32), pltpu.VMEM((2 * r, m), BF16)],
        compiler_params=limit(6),
        cost_estimate=NO_COST,
        name="core_rows",
    )(place, mine, other, wide)


def factor_kernel(scale, place_ref, mine_ref, other_ref, start_ref, tri_ref, basis_ref, full_ref, inv_ref, up_ref):
    m = full_ref.shape[0]
    nblk = m // NB

    def sl(i):
        return slice(i * NB, (i + 1) * NB)

    share = mine_ref.shape[0] // NB

    def block(halves, i, j):
        b = block_index(i, j)
        return halves[b // share][sl(b % share), :] * scale

    @pl.when(place_ref[1] == 0)
    def _():
        for i in range(nblk):
            for j in range(i + 1):
                full_ref[sl(i), sl(j)] = block((mine_ref, other_ref), i, j)

        def panel(p, carry):
            here = pl.ds(pl.multiple_of(p * NB, NB), NB)
            cholesky_block(full_ref[here, here], inv_ref, up_ref)
            column = dot_exact(full_ref[:, here], inv_ref[...], NT)
            row = lax.broadcasted_iota(jnp.int32, column.shape, 0)
            below = jnp.where(row >= (p + 1) * NB, column, 0.0)
            full_ref[:, here] = below

            @pl.when(p + 1 < nblk)
            def _():
                for j in range(1, nblk):
                    @pl.when(p < j)
                    def _():
                        full_ref[j * NB :, sl(j)] -= dot_exact(below[j * NB :, :], below[sl(j), :], NT)

            full_ref[here, here] = up_ref[...].T
            return carry

        lax.fori_loop(0, nblk, panel, 0)
        for i in range(nblk):
            for j in range(i + 1):
                tri_ref[sl(block_index(i, j)), :] = full_ref[sl(i), sl(j)]

    @pl.when(place_ref[1] != 0)
    def _():
        for i in range(nblk):
            for j in range(i + 1):
                b = block((other_ref, mine_ref), i, j)
                full_ref[sl(i), sl(j)] = b
                if j < i:
                    full_ref[sl(j), sl(i)] = b.T
        basis_ref[...] = start_ref[...]

        def step(_, carry):
            image = dot_exact(full_ref[...], basis_ref[...])
            cholesky_block(dot_exact(image, image, TN), inv_ref)
            basis_ref[...] = dot_exact(image, inv_ref[...], NT)
            return carry

        lax.fori_loop(0, ITERS, step, 0)


def factorize(place, mine, other, start_block, scale):
    m, r = start_block.shape
    packed = (2 * mine.shape[0], NB)
    return pl.pallas_call(
        functools.partial(factor_kernel, scale),
        in_specs=[SMEM, VMEM, VMEM, VMEM],
        out_specs=[VMEM, VMEM],
        out_shape=[jax.ShapeDtypeStruct(packed, F32), jax.ShapeDtypeStruct((m, r), F32)],
        scratch_shapes=[pltpu.VMEM((m, m), F32), pltpu.VMEM((NB, NB), F32), pltpu.VMEM((NB, NB), F32)],
        compiler_params=limit(8),
        cost_estimate=NO_COST,
        name="factorize",
    )(place, mine, other, start_block)


def unpack_kernel(place_ref, mine_ref, other_ref, tri_ref):
    nblk = tri_ref.shape[0] // NB

    def fill(source):
        for i in range(nblk):
            for j in range(nblk):
                b = block_index(i, j)
                value = source[b * NB : (b + 1) * NB, :] if j <= i else jnp.zeros((NB, NB), F32)
                tri_ref[i * NB : (i + 1) * NB, j * NB : (j + 1) * NB] = value

    pl.when(place_ref[1] == 0)(lambda: fill(mine_ref))
    pl.when(place_ref[1] != 0)(lambda: fill(other_ref))


def unpack_triangle(place, mine, other):
    m = MODE * NB
    return pl.pallas_call(
        unpack_kernel,
        in_specs=[SMEM, VMEM, VMEM],
        out_specs=VMEM,
        out_shape=jax.ShapeDtypeStruct((m, m), F32),
        compiler_params=limit(4),
        cost_estimate=NO_COST,
        name="unpack_triangle",
    )(place, mine, other)


def swap_cores(value):
    return lax.ppermute(value, "core", [(0, 1), (1, 0)])


def shift(value, axis, by):
    n = lax.axis_size(axis)
    return lax.ppermute(value, axis, [(i, (i + by) % n) for i in range(n)])


def spread_out(value, axes):
    n = lax.axis_size(axes)
    copies = jnp.broadcast_to(value[None], (n,) + value.shape)
    return lax.all_to_all(copies, axes, 0, 0, tiled=True)


def sum_z(value):
    value = value + lax.ppermute(value, "z", [(i, i ^ 1) for i in range(8)])
    side, back, other = (shift(value, "z", 2), shift(value, "z", 6), shift(value, "z", 4))
    return (value + other) + (side + back)


def sum_everywhere(mine, other):
    rows, lanes = mine.shape
    mine = mine + swap_cores(other)
    plane = ("mode", "y")
    n = lax.axis_size(plane)
    pieces = lax.all_to_all(mine.reshape(n, rows // n, lanes), plane, 0, 0, tiled=True)
    piece = sum_z(pieces.sum(0))
    mine = spread_out(piece, plane).reshape(rows, lanes)
    return mine, swap_cores(mine)


def per_device(unfolded, start_block):
    total_cols = unfolded.shape[1] * lax.axis_size(("y", "z", "core"))
    position, core_id = lax.axis_index("mode"), lax.axis_index("core")
    place = jnp.stack([position, core_id]).astype(jnp.int32)
    share = unfolded.shape[1] // MODE
    starts = [sum(WIDTHS[:c]) for c in range(len(WIDTHS))]

    def columns(k, width):
        owner = ((position + k) & (MODE - 1)).astype(jnp.uint32)
        return lax.dynamic_slice_in_dim(unfolded, owner * share, width, axis=1)

    received, source = [], unfolded
    for start, width in zip(starts, WIDTHS):
        if start == 0:
            sent = {k: columns(k, width) for k in (2, 1, 3)}
        else:
            sent = dict(zip((2, 1, 3), column_slices(place, source, (2, 1, 3), start, width)))
        source, _ = lax.optimization_barrier((source, sent[2]))
        received.append([shift(sent[k], "mode", k) for k in range(1, MODE)])
    own = [column_slices(place, source, (0,), start, width)[0] for start, width in zip(starts, WIDTHS)]
    sums, wides = [None], []
    for c in range(len(WIDTHS)):
        wide, *sums = gram_lower(place, [own[c]] + received[c], sums[0], c == len(WIDTHS) - 1)
        wides.append(wide)
    sums = sum_everywhere(*sums)
    tri, basis = factorize(place, *sums, start_block, 1.0 / total_cols)
    basis_there = swap_cores(basis)
    factor = jnp.where(core_id == 1, basis, basis_there)
    triangle = unpack_triangle(place, tri, swap_cores(tri))
    landed = []
    for c, wide in enumerate(wides):
        parts = core_rows(place, basis, basis_there, wide)
        for k in (2, 1, 3, 0):
            got = shift(parts[k], "mode", k) if k else parts[0]
            landed.append((((position - k) & (MODE - 1)) * share + starts[c], got))
    core = jnp.zeros((factor.shape[1] // MODE, MODE * share), F32)
    core, triangle, factor, _ = lax.optimization_barrier((core, triangle, factor, parts[0]))
    for at, got in landed:
        core = lax.dynamic_update_slice_in_dim(core, got, at, axis=1)
    return (triangle, factor, core)


def solution(mesh):
    fine = Mesh(mesh.devices.reshape(4, 4, 8, 2), ("mode", "y", "z", "core"))
    rest = ("y", "z", "core")
    return jax.shard_map(
        per_device,
        mesh=fine,
        in_specs=(P("mode", rest), P()),
        out_specs=(P(), P(), P("mode", rest)),
        check_vma=False,
    )
```

```python
import functools

import jax
import jax.numpy as jnp
from jax import lax
from jax.experimental import pallas as pl
from jax.experimental.pallas import tpu as pltpu
from jax.sharding import Mesh, PartitionSpec as P

ITERS = 3
MODE = 4
WIDTHS = (1024, 1024)
TILE = 512
HIGHEST = lax.Precision.HIGHEST
NB = 128
NT = (((1,), (1,)), ((), ()))
TN = (((0,), (0,)), ((), ()))
F32 = jnp.float32


def dot_exact(a, b, dims=(((1,), (0,)), ((), ()))):
    return lax.dot_general(a, b, dims, precision=HIGHEST, preferred_element_type=F32)


def cholesky_block(matrix, inverse_ref, upper_ref=None):
    n = matrix.shape[0]
    shape = (8, n)
    spread = functools.partial(jnp.broadcast_to, shape=shape)
    lane = lax.broadcasted_iota(jnp.int32, shape, 1)
    sub = lax.broadcasted_iota(jnp.int32, shape, 0)
    rows = [matrix[8 * i : 8 * i + 8, :] for i in range(n // 8)]
    for t in range(n // 8):
        first = 8 * t
        inside = (lane >= first) & (lane < first + 8)
        cols = {
            i: [spread(rows[i][:, first + j : first + j + 1]) for j in range(8)]
            for i in range(t, n // 8)
        }
        own = cols[t]
        top = rows[t]
        unit = jnp.where(lane == first + sub, 1.0, 0.0)
        recips = []
        left = {i: jnp.where(inside, 0.0, rows[i]) for i in range(t + 1, n // 8)}
        for j in range(8):
            recip = 1.0 / spread(own[j][j : j + 1, :])
            recips.append(recip)
            source = spread(jnp.where(inside, unit, top)[j : j + 1, :])
            mult = jnp.where(sub > j, own[j] * recip, 0.0)
            top = top - mult * spread(top[j : j + 1, :])
            unit = unit - mult * spread(unit[j : j + 1, :])
            pivot_row = {l: spread(own[l][j : j + 1, :]) for l in range(j + 1, 8)}
            for i in range(t + 1, n // 8):
                mult = cols[i][j] * recip
                left[i] = left[i] - mult * source
                for l in range(j + 1, 8):
                    cols[i][l] = cols[i][l] - mult * pivot_row[l]
            for l in range(j + 1, 8):
                own[l] = own[l] - (own[j] * pivot_row[l]) * recip
        scale = recips[0]
        for j in range(1, 8):
            scale = jnp.where(sub == j, recips[j], scale)
        scale = lax.rsqrt(1.0 / scale)
        inverse_ref[first : first + 8, :] = scale * jnp.where(lane < first, top, unit)
        if upper_ref is not None:
            upper_ref[first : first + 8, :] = jnp.where(lane >= first + sub, scale * top, 0.0)
        rows[t + 1 :] = [left[i] for i in range(t + 1, n // 8)]


def block_index(i, j):
    return i * (i + 1) // 2 + j


VMEM = pl.BlockSpec(memory_space=pltpu.VMEM)
SMEM = pl.BlockSpec(memory_space=pltpu.SMEM)
BF16 = jnp.bfloat16
NO_COST = pl.CostEstimate(flops=0, transcendentals=0, bytes_accessed=0)


def limit(mib):
    return pltpu.CompilerParams(vmem_limit_bytes=mib << 20)


def high_low(value):
    high = value.astype(BF16)
    return high, (value - high.astype(F32)).astype(BF16)


def slice_kernel(shifts, start, share, place_ref, source_ref, *refs):
    outs, sem = refs[:-1], refs[-1]
    width = outs[0].shape[1]
    copies = []
    for n, k in enumerate(shifts):
        at = pl.multiple_of(((place_ref[0] + k) & (MODE - 1)) * share + start, NB)
        copies.append(pltpu.make_async_copy(source_ref.at[:, pl.ds(at, width)], outs[n], sem.at[n]))
        copies[-1].start()
    for copy in copies:
        copy.wait()


def column_slices(place, source, shifts, start, width):
    rows, cols = source.shape
    return pl.pallas_call(
        functools.partial(slice_kernel, shifts, start, cols // MODE),
        in_specs=[SMEM, pl.BlockSpec(memory_space=pl.ANY)],
        out_specs=[VMEM] * len(shifts),
        out_shape=[jax.ShapeDtypeStruct((rows, width), F32)] * len(shifts),
        scratch_shapes=[pltpu.SemaphoreType.DMA((len(shifts),))],
        compiler_params=limit(4),
        cost_estimate=NO_COST,
        name="column_slices",
    )(place, source)


def gram_kernel(has_prior, final, place_ref, *refs):
    pieces, refs = refs[:MODE], refs[MODE:]
    prior_ref, refs = (refs[0], refs[1:]) if has_prior else (None, refs)
    wide_ref, outs, acc_ref = refs[0], refs[1:-1], refs[-1]
    m = acc_ref.shape[0]
    half = m // 2
    cols = pieces[0].shape[1]
    upper, lower, whole = slice(0, half), slice(half, m), slice(0, m)
    dot = functools.partial(lax.dot_general, dimension_numbers=NT, preferred_element_type=F32)
    for t in range(cols // TILE):
        for k, piece in enumerate(pieces):
            rows = pl.ds(pl.multiple_of(((place_ref[0] - k) & (MODE - 1)) * NB, NB), NB)
            high, low = high_low(piece[:, t * TILE : (t + 1) * TILE])
            wide_ref[rows, 2 * t * TILE : (2 * t + 1) * TILE] = high
            wide_ref[rows, (2 * t + 1) * TILE : (2 * t + 2) * TILE] = low

        def product(r, c):
            left = wide_ref[r, 2 * t * TILE : (2 * t + 2) * TILE]
            high = wide_ref[c, 2 * t * TILE : (2 * t + 1) * TILE]
            low = wide_ref[c, (2 * t + 1) * TILE : (2 * t + 2) * TILE]
            straight, turned = jnp.concatenate([high, low], axis=1), jnp.concatenate([low, high], axis=1)
            return dot(left, straight) + dot(left, turned)

        if t == 0:
            acc_ref[upper, upper] = product(upper, upper)
            acc_ref[lower, whole] = product(lower, whole)
        else:
            acc_ref[upper, upper] += product(upper, upper)
            acc_ref[lower, whole] += product(lower, whole)

    share = outs[0].shape[0] // NB

    def write(first, second):
        for i in range(m // NB):
            for j in range(i + 1):
                b = block_index(i, j)
                value = acc_ref[i * NB : (i + 1) * NB, j * NB : (j + 1) * NB]
                if prior_ref is not None:
                    value = value + prior_ref[b * NB : (b + 1) * NB, :]
                target = first if b < share else second
                target[b % share * NB : (b % share + 1) * NB, :] = value

    if final:
        pl.when(place_ref[1] == 0)(lambda: write(outs[0], outs[1]))
        pl.when(place_ref[1] != 0)(lambda: write(outs[1], outs[0]))
    else:
        write(outs[0], None)


def gram_lower(place, pieces, prior, final):
    rows, cols = pieces[0].shape
    m = rows * MODE
    rows_out = MODE * (MODE + 1) // 2 * NB
    priors = [] if prior is None else [prior]
    heights = [rows_out // 2] * 2 if final else [rows_out]
    return pl.pallas_call(
        functools.partial(gram_kernel, prior is not None, final),
        in_specs=[SMEM] + [VMEM] * (MODE + len(priors)),
        out_specs=[VMEM] * (1 + len(heights)),
        out_shape=[jax.ShapeDtypeStruct((m, 2 * cols), BF16)] + [jax.ShapeDtypeStruct((h, NB), F32) for h in heights],
        scratch_shapes=[pltpu.VMEM((m, m), F32)],
        compiler_params=limit(8),
        cost_estimate=NO_COST,
        name="gram_lower",
    )(place, *pieces, *priors)


def core_kernel(place_ref, mine_ref, other_ref, wide_ref, *refs):
    outs, (result_ref, turned_ref) = refs[:MODE], refs[MODE:]
    r = mine_ref.shape[1]
    factor = jnp.where(place_ref[1] == 1, mine_ref[...], other_ref[...])
    turned_ref[:r, :], turned_ref[r:, :] = high_low(factor.T)
    for t in range(wide_ref.shape[1] // (2 * TILE)):
        both = jnp.dot(turned_ref[...], wide_ref[:, 2 * t * TILE : (2 * t + 2) * TILE], preferred_element_type=F32)
        big, small = both[:, :TILE], both[:, TILE:]
        result_ref[:, t * TILE : (t + 1) * TILE] = big[:r, :] + (big[r:, :] + (small[:r, :] + small[r:, :]))
    share = outs[0].shape[0]
    for k, out in enumerate(outs):
        at = pl.multiple_of(((place_ref[0] + k) & (MODE - 1)) * share, share)
        out[...] = result_ref[pl.ds(at, share), :]


def core_rows(place, mine, other, wide):
    m, r = mine.shape
    cols = wide.shape[1] // 2
    return pl.pallas_call(
        core_kernel,
        in_specs=[SMEM] + [VMEM] * 3,
        out_specs=[VMEM] * MODE,
        out_shape=[jax.ShapeDtypeStruct((r // MODE, cols), F32)] * MODE,
        scratch_shapes=[pltpu.VMEM((r, cols), F32), pltpu.VMEM((2 * r, m), BF16)],
        compiler_params=limit(6),
        cost_estimate=NO_COST,
        name="core_rows",
    )(place, mine, other, wide)


def factor_kernel(scale, place_ref, mine_ref, other_ref, start_ref, tri_ref, basis_ref, full_ref, inv_ref, up_ref):
    m = full_ref.shape[0]
    nblk = m // NB

    def sl(i):
        return slice(i * NB, (i + 1) * NB)

    share = mine_ref.shape[0] // NB

    def block(halves, i, j):
        b = block_index(i, j)
        return halves[b // share][sl(b % share), :] * scale

    @pl.when(place_ref[1] == 0)
    def _():
        for i in range(nblk):
            for j in range(i + 1):
                full_ref[sl(i), sl(j)] = block((mine_ref, other_ref), i, j)

        def panel(p, carry):
            here = pl.ds(pl.multiple_of(p * NB, NB), NB)
            cholesky_block(full_ref[here, here], inv_ref, up_ref)
            column = dot_exact(full_ref[:, here], inv_ref[...], NT)
            row = lax.broadcasted_iota(jnp.int32, column.shape, 0)
            below = jnp.where(row >= (p + 1) * NB, column, 0.0)
            full_ref[:, here] = below

            @pl.when(p + 1 < nblk)
            def _():
                for j in range(1, nblk):
                    @pl.when(p < j)
                    def _():
                        full_ref[j * NB :, sl(j)] -= dot_exact(below[j * NB :, :], below[sl(j), :], NT)

            full_ref[here, here] = up_ref[...].T
            return carry

        lax.fori_loop(0, nblk, panel, 0)
        for i in range(nblk):
            for j in range(i + 1):
                tri_ref[sl(block_index(i, j)), :] = full_ref[sl(i), sl(j)]

    @pl.when(place_ref[1] != 0)
    def _():
        for i in range(nblk):
            for j in range(i + 1):
                b = block((other_ref, mine_ref), i, j)
                full_ref[sl(i), sl(j)] = b
                if j < i:
                    full_ref[sl(j), sl(i)] = b.T
        basis_ref[...] = start_ref[...]

        def step(_, carry):
            image = dot_exact(full_ref[...], basis_ref[...])
            cholesky_block(dot_exact(image, image, TN), inv_ref)
            basis_ref[...] = dot_exact(image, inv_ref[...], NT)
            return carry

        lax.fori_loop(0, ITERS, step, 0)


def factorize(place, mine, other, start_block, scale):
    m, r = start_block.shape
    packed = (2 * mine.shape[0], NB)
    return pl.pallas_call(
        functools.partial(factor_kernel, scale),
        in_specs=[SMEM, VMEM, VMEM, VMEM],
        out_specs=[VMEM, VMEM],
        out_shape=[jax.ShapeDtypeStruct(packed, F32), jax.ShapeDtypeStruct((m, r), F32)],
        scratch_shapes=[pltpu.VMEM((m, m), F32), pltpu.VMEM((NB, NB), F32), pltpu.VMEM((NB, NB), F32)],
        compiler_params=limit(8),
        cost_estimate=NO_COST,
        name="factorize",
    )(place, mine, other, start_block)


def unpack_kernel(place_ref, mine_ref, other_ref, tri_ref):
    nblk = tri_ref.shape[0] // NB

    def fill(source):
        for i in range(nblk):
            for j in range(nblk):
                b = block_index(i, j)
                value = source[b * NB : (b + 1) * NB, :] if j <= i else jnp.zeros((NB, NB), F32)
                tri_ref[i * NB : (i + 1) * NB, j * NB : (j + 1) * NB] = value

    pl.when(place_ref[1] == 0)(lambda: fill(mine_ref))
    pl.when(place_ref[1] != 0)(lambda: fill(other_ref))


def unpack_triangle(place, mine, other):
    m = MODE * NB
    return pl.pallas_call(
        unpack_kernel,
        in_specs=[SMEM, VMEM, VMEM],
        out_specs=VMEM,
        out_shape=jax.ShapeDtypeStruct((m, m), F32),
        compiler_params=limit(4),
        cost_estimate=NO_COST,
        name="unpack_triangle",
    )(place, mine, other)


def swap_cores(value):
    return lax.ppermute(value, "core", [(0, 1), (1, 0)])


def shift(value, axis, by):
    n = lax.axis_size(axis)
    return lax.ppermute(value, axis, [(i, (i + by) % n) for i in range(n)])


def spread_out(value, axes):
    n = lax.axis_size(axes)
    copies = jnp.broadcast_to(value[None], (n,) + value.shape)
    return lax.all_to_all(copies, axes, 0, 0, tiled=True)


def sum_z(value):
    value = value + lax.ppermute(value, "z", [(i, i ^ 1) for i in range(8)])
    side, back, other = (shift(value, "z", 2), shift(value, "z", 6), shift(value, "z", 4))
    return (value + other) + (side + back)


def sum_everywhere(mine, other):
    rows, lanes = mine.shape
    mine = mine + swap_cores(other)
    plane = ("mode", "y")
    n = lax.axis_size(plane)
    pieces = lax.all_to_all(mine.reshape(n, rows // n, lanes), plane, 0, 0, tiled=True)
    piece = sum_z(pieces.sum(0))
    mine = spread_out(piece, plane).reshape(rows, lanes)
    return mine, swap_cores(mine)


def per_device(unfolded, start_block):
    total_cols = unfolded.shape[1] * lax.axis_size(("y", "z", "core"))
    position, core_id = lax.axis_index("mode"), lax.axis_index("core")
    place = jnp.stack([position, core_id]).astype(jnp.int32)
    share = unfolded.shape[1] // MODE
    starts = [sum(WIDTHS[:c]) for c in range(len(WIDTHS))]

    def columns(k, width):
        owner = ((position + k) & (MODE - 1)).astype(jnp.uint32)
        return lax.dynamic_slice_in_dim(unfolded, owner * share, width, axis=1)

    received, source = [], unfolded
    for start, width in zip(starts, WIDTHS):
        if start == 0:
            sent = {k: columns(k, width) for k in (2, 1, 3)}
        else:
            sent = dict(zip((2, 1, 3), column_slices(place, source, (2, 1, 3), start, width)))
        source, _ = lax.optimization_barrier((source, sent[2]))
        received.append([shift(sent[k], "mode", k) for k in range(1, MODE)])
    own = [column_slices(place, source, (0,), start, width)[0] for start, width in zip(starts, WIDTHS)]
    sums, wides = [None], []
    for c in range(len(WIDTHS)):
        wide, *sums = gram_lower(place, [own[c]] + received[c], sums[0], c == len(WIDTHS) - 1)
        wides.append(wide)
    sums = sum_everywhere(*sums)
    tri, basis = factorize(place, *sums, start_block, 1.0 / total_cols)
    basis_there = swap_cores(basis)
    factor = jnp.where(core_id == 1, basis, basis_there)
    triangle = unpack_triangle(place, tri, swap_cores(tri))
    landed = []
    for c, wide in enumerate(wides):
        parts = core_rows(place, basis, basis_there, wide)
        for k in (2, 1, 3, 0):
            got = shift(parts[k], "mode", k) if k else parts[0]
            landed.append((((position - k) & (MODE - 1)) * share + starts[c], got))
    core = jnp.zeros((factor.shape[1] // MODE, MODE * share), F32)
    core, triangle, factor, _ = lax.optimization_barrier((core, triangle, factor, parts[0]))
    for at, got in landed:
        core = lax.dynamic_update_slice_in_dim(core, got, at, axis=1)
    return (triangle, factor, core)


def solution(mesh):
    fine = Mesh(mesh.devices.reshape(4, 4, 8, 2), ("mode", "y", "z", "core"))
    rest = ("y", "z", "core")
    return jax.shard_map(
        per_device,
        mesh=fine,
        in_specs=(P("mode", rest), P()),
        out_specs=(P(), P(), P("mode", rest)),
        check_vma=False,
    )
```

```python
import functools

import jax
import jax.numpy as jnp
from jax import lax
from jax.experimental import pallas as pl
from jax.experimental.pallas import tpu as pltpu
from jax.sharding import Mesh, PartitionSpec as P

ITERS = 3
MODE = 4
WIDTHS = (1024, 1024)
TILE = 512
HIGHEST = lax.Precision.HIGHEST
NB = 128
NT = (((1,), (1,)), ((), ()))
TN = (((0,), (0,)), ((), ()))
F32 = jnp.float32


def dot_exact(a, b, dims=(((1,), (0,)), ((), ()))):
    return lax.dot_general(a, b, dims, precision=HIGHEST, preferred_element_type=F32)


def cholesky_block(matrix, inverse_ref, upper_ref=None):
    n = matrix.shape[0]
    shape = (8, n)
    spread = functools.partial(jnp.broadcast_to, shape=shape)
    lane = lax.broadcasted_iota(jnp.int32, shape, 1)
    sub = lax.broadcasted_iota(jnp.int32, shape, 0)
    rows = [matrix[8 * i : 8 * i + 8, :] for i in range(n // 8)]
    for t in range(n // 8):
        first = 8 * t
        inside = (lane >= first) & (lane < first + 8)
        cols = {
            i: [spread(rows[i][:, first + j : first + j + 1]) for j in range(8)]
            for i in range(t, n // 8)
        }
        own = cols[t]
        top = rows[t]
        unit = jnp.where(lane == first + sub, 1.0, 0.0)
        recips = []
        left = {i: jnp.where(inside, 0.0, rows[i]) for i in range(t + 1, n // 8)}
        for j in range(8):
            recip = 1.0 / spread(own[j][j : j + 1, :])
            recips.append(recip)
            source = spread(jnp.where(inside, unit, top)[j : j + 1, :])
            mult = jnp.where(sub > j, own[j] * recip, 0.0)
            top = top - mult * spread(top[j : j + 1, :])
            unit = unit - mult * spread(unit[j : j + 1, :])
            pivot_row = {l: spread(own[l][j : j + 1, :]) for l in range(j + 1, 8)}
            for i in range(t + 1, n // 8):
                mult = cols[i][j] * recip
                left[i] = left[i] - mult * source
                for l in range(j + 1, 8):
                    cols[i][l] = cols[i][l] - mult * pivot_row[l]
            for l in range(j + 1, 8):
                own[l] = own[l] - (own[j] * pivot_row[l]) * recip
        scale = recips[0]
        for j in range(1, 8):
            scale = jnp.where(sub == j, recips[j], scale)
        scale = lax.rsqrt(1.0 / scale)
        inverse_ref[first : first + 8, :] = scale * jnp.where(lane < first, top, unit)
        if upper_ref is not None:
            upper_ref[first : first + 8, :] = jnp.where(lane >= first + sub, scale * top, 0.0)
        rows[t + 1 :] = [left[i] for i in range(t + 1, n // 8)]


def block_index(i, j):
    return i * (i + 1) // 2 + j


VMEM = pl.BlockSpec(memory_space=pltpu.VMEM)
SMEM = pl.BlockSpec(memory_space=pltpu.SMEM)
BF16 = jnp.bfloat16
NO_COST = pl.CostEstimate(flops=0, transcendentals=0, bytes_accessed=0)


def limit(mib):
    return pltpu.CompilerParams(vmem_limit_bytes=mib << 20)


def high_low(value):
    high = value.astype(BF16)
    return high, (value - high.astype(F32)).astype(BF16)


def slice_kernel(shifts, start, share, place_ref, source_ref, *refs):
    outs, sem = refs[:-1], refs[-1]
    width = outs[0].shape[1]
    copies = []
    for n, k in enumerate(shifts):
        at = pl.multiple_of(((place_ref[0] + k) & (MODE - 1)) * share + start, NB)
        copies.append(pltpu.make_async_copy(source_ref.at[:, pl.ds(at, width)], outs[n], sem.at[n]))
        copies[-1].start()
    for copy in copies:
        copy.wait()


def column_slices(place, source, shifts, start, width):
    rows, cols = source.shape
    return pl.pallas_call(
        functools.partial(slice_kernel, shifts, start, cols // MODE),
        in_specs=[SMEM, pl.BlockSpec(memory_space=pl.ANY)],
        out_specs=[VMEM] * len(shifts),
        out_shape=[jax.ShapeDtypeStruct((rows, width), F32)] * len(shifts),
        scratch_shapes=[pltpu.SemaphoreType.DMA((len(shifts),))],
        compiler_params=limit(4),
        cost_estimate=NO_COST,
        name="column_slices",
    )(place, source)


def gram_kernel(has_prior, final, place_ref, *refs):
    pieces, refs = refs[:MODE], refs[MODE:]
    prior_ref, refs = (refs[0], refs[1:]) if has_prior else (None, refs)
    wide_ref, outs, acc_ref = refs[0], refs[1:-1], refs[-1]
    m = acc_ref.shape[0]
    half = m // 2
    cols = pieces[0].shape[1]
    upper, lower, whole = slice(0, half), slice(half, m), slice(0, m)
    dot = functools.partial(lax.dot_general, dimension_numbers=NT, preferred_element_type=F32)
    for t in range(cols // TILE):
        for k, piece in enumerate(pieces):
            rows = pl.ds(pl.multiple_of(((place_ref[0] - k) & (MODE - 1)) * NB, NB), NB)
            high, low = high_low(piece[:, t * TILE : (t + 1) * TILE])
            wide_ref[rows, 2 * t * TILE : (2 * t + 1) * TILE] = high
            wide_ref[rows, (2 * t + 1) * TILE : (2 * t + 2) * TILE] = low

        def product(r, c):
            left = wide_ref[r, 2 * t * TILE : (2 * t + 2) * TILE]
            high = wide_ref[c, 2 * t * TILE : (2 * t + 1) * TILE]
            low = wide_ref[c, (2 * t + 1) * TILE : (2 * t + 2) * TILE]
            straight, turned = jnp.concatenate([high, low], axis=1), jnp.concatenate([low, high], axis=1)
            return dot(left, straight) + dot(left, turned)

        if t == 0:
            acc_ref[upper, upper] = product(upper, upper)
            acc_ref[lower, whole] = product(lower, whole)
        else:
            acc_ref[upper, upper] += product(upper, upper)
            acc_ref[lower, whole] += product(lower, whole)

    share = outs[0].shape[0] // NB

    def write(first, second):
        for i in range(m // NB):
            for j in range(i + 1):
                b = block_index(i, j)
                value = acc_ref[i * NB : (i + 1) * NB, j * NB : (j + 1) * NB]
                if prior_ref is not None:
                    value = value + prior_ref[b * NB : (b + 1) * NB, :]
                target = first if b < share else second
                target[b % share * NB : (b % share + 1) * NB, :] = value

    if final:
        pl.when(place_ref[1] == 0)(lambda: write(outs[0], outs[1]))
        pl.when(place_ref[1] != 0)(lambda: write(outs[1], outs[0]))
    else:
        write(outs[0], None)


def gram_lower(place, pieces, prior, final):
    rows, cols = pieces[0].shape
    m = rows * MODE
    rows_out = MODE * (MODE + 1) // 2 * NB
    priors = [] if prior is None else [prior]
    heights = [rows_out // 2] * 2 if final else [rows_out]
    return pl.pallas_call(
        functools.partial(gram_kernel, prior is not None, final),
        in_specs=[SMEM] + [VMEM] * (MODE + len(priors)),
        out_specs=[VMEM] * (1 + len(heights)),
        out_shape=[jax.ShapeDtypeStruct((m, 2 * cols), BF16)] + [jax.ShapeDtypeStruct((h, NB), F32) for h in heights],
        scratch_shapes=[pltpu.VMEM((m, m), F32)],
        compiler_params=limit(8),
        cost_estimate=NO_COST,
        name="gram_lower",
    )(place, *pieces, *priors)


def core_kernel(place_ref, mine_ref, other_ref, wide_ref, *refs):
    outs, (result_ref, turned_ref) = refs[:MODE], refs[MODE:]
    r = mine_ref.shape[1]
    factor = jnp.where(place_ref[1] == 1, mine_ref[...], other_ref[...])
    turned_ref[:r, :], turned_ref[r:, :] = high_low(factor.T)
    for t in range(wide_ref.shape[1] // (2 * TILE)):
        both = jnp.dot(turned_ref[...], wide_ref[:, 2 * t * TILE : (2 * t + 2) * TILE], preferred_element_type=F32)
        big, small = both[:, :TILE], both[:, TILE:]
        result_ref[:, t * TILE : (t + 1) * TILE] = big[:r, :] + (big[r:, :] + (small[:r, :] + small[r:, :]))
    share = outs[0].shape[0]
    for k, out in enumerate(outs):
        at = pl.multiple_of(((place_ref[0] + k) & (MODE - 1)) * share, share)
        out[...] = result_ref[pl.ds(at, share), :]


def core_rows(place, mine, other, wide):
    m, r = mine.shape
    cols = wide.shape[1] // 2
    return pl.pallas_call(
        core_kernel,
        in_specs=[SMEM] + [VMEM] * 3,
        out_specs=[VMEM] * MODE,
        out_shape=[jax.ShapeDtypeStruct((r // MODE, cols), F32)] * MODE,
        scratch_shapes=[pltpu.VMEM((r, cols), F32), pltpu.VMEM((2 * r, m), BF16)],
        compiler_params=limit(6),
        cost_estimate=NO_COST,
        name="core_rows",
    )(place, mine, other, wide)


def factor_kernel(scale, place_ref, mine_ref, other_ref, start_ref, tri_ref, basis_ref, full_ref, inv_ref, up_ref):
    m = full_ref.shape[0]
    nblk = m // NB

    def sl(i):
        return slice(i * NB, (i + 1) * NB)

    share = mine_ref.shape[0] // NB

    def block(halves, i, j):
        b = block_index(i, j)
        return halves[b // share][sl(b % share), :] * scale

    @pl.when(place_ref[1] == 0)
    def _():
        for i in range(nblk):
            for j in range(i + 1):
                full_ref[sl(i), sl(j)] = block((mine_ref, other_ref), i, j)

        def panel(p, carry):
            here = pl.ds(pl.multiple_of(p * NB, NB), NB)
            cholesky_block(full_ref[here, here], inv_ref, up_ref)
            column = dot_exact(full_ref[NB:, here], inv_ref[...], NT)
            row = lax.broadcasted_iota(jnp.int32, column.shape, 0)
            below = jnp.where(row >= p * NB, column, 0.0)
            full_ref[NB:, here] = below

            @pl.when(p + 1 < nblk)
            def _():
                for j in range(1, nblk):
                    @pl.when(p < j)
                    def _():
                        full_ref[j * NB :, sl(j)] -= dot_exact(below[(j - 1) * NB :, :], below[sl(j - 1), :], NT)

            full_ref[here, here] = up_ref[...].T
            return carry

        lax.fori_loop(0, nblk, panel, 0)
        for i in range(nblk):
            for j in range(i + 1):
                tri_ref[sl(block_index(i, j)), :] = full_ref[sl(i), sl(j)]

    @pl.when(place_ref[1] != 0)
    def _():
        for i in range(nblk):
            for j in range(i + 1):
                b = block((other_ref, mine_ref), i, j)
                full_ref[sl(i), sl(j)] = b
                if j < i:
                    full_ref[sl(j), sl(i)] = b.T
        basis_ref[...] = dot_exact(full_ref[...], start_ref[...])

        def step(n, carry):
            image = basis_ref[...]
            projected = dot_exact(image, image, TN)
            ahead = dot_exact(full_ref[...], image)
            cholesky_block(projected, inv_ref)
            last = n == ITERS - 1
            basis_ref[...] = dot_exact(jnp.where(last, image, ahead), inv_ref[...], NT)
            return carry

        lax.fori_loop(0, ITERS, step, 0)


def factorize(place, mine, other, start_block, scale):
    m, r = start_block.shape
    packed = (2 * mine.shape[0], NB)
    return pl.pallas_call(
        functools.partial(factor_kernel, scale),
        in_specs=[SMEM, VMEM, VMEM, VMEM],
        out_specs=[VMEM, VMEM],
        out_shape=[jax.ShapeDtypeStruct(packed, F32), jax.ShapeDtypeStruct((m, r), F32)],
        scratch_shapes=[pltpu.VMEM((m, m), F32), pltpu.VMEM((NB, NB), F32), pltpu.VMEM((NB, NB), F32)],
        compiler_params=limit(8),
        cost_estimate=NO_COST,
        name="factorize",
    )(place, mine, other, start_block)


def unpack_kernel(place_ref, mine_ref, other_ref, tri_ref):
    nblk = tri_ref.shape[0] // NB

    def fill(source):
        for i in range(nblk):
            for j in range(nblk):
                b = block_index(i, j)
                value = source[b * NB : (b + 1) * NB, :] if j <= i else jnp.zeros((NB, NB), F32)
                tri_ref[i * NB : (i + 1) * NB, j * NB : (j + 1) * NB] = value

    pl.when(place_ref[1] == 0)(lambda: fill(mine_ref))
    pl.when(place_ref[1] != 0)(lambda: fill(other_ref))


def unpack_triangle(place, mine, other):
    m = MODE * NB
    return pl.pallas_call(
        unpack_kernel,
        in_specs=[SMEM, VMEM, VMEM],
        out_specs=VMEM,
        out_shape=jax.ShapeDtypeStruct((m, m), F32),
        compiler_params=limit(4),
        cost_estimate=NO_COST,
        name="unpack_triangle",
    )(place, mine, other)


def swap_cores(value):
    return lax.ppermute(value, "core", [(0, 1), (1, 0)])


def shift(value, axis, by):
    n = lax.axis_size(axis)
    return lax.ppermute(value, axis, [(i, (i + by) % n) for i in range(n)])


def spread_out(value, axes):
    n = lax.axis_size(axes)
    copies = jnp.broadcast_to(value[None], (n,) + value.shape)
    return lax.all_to_all(copies, axes, 0, 0, tiled=True)


def sum_z(value):
    value = value + lax.ppermute(value, "z", [(i, i ^ 1) for i in range(8)])
    side, back, other = (shift(value, "z", 2), shift(value, "z", 6), shift(value, "z", 4))
    return (value + other) + (side + back)


def sum_everywhere(mine, other):
    rows, lanes = mine.shape
    mine = mine + swap_cores(other)
    plane = ("mode", "y")
    n = lax.axis_size(plane)
    pieces = lax.all_to_all(mine.reshape(n, rows // n, lanes), plane, 0, 0, tiled=True)
    piece = sum_z(pieces.sum(0))
    mine = spread_out(piece, plane).reshape(rows, lanes)
    return mine, swap_cores(mine)


def per_device(unfolded, start_block):
    total_cols = unfolded.shape[1] * lax.axis_size(("y", "z", "core"))
    position, core_id = lax.axis_index("mode"), lax.axis_index("core")
    place = jnp.stack([position, core_id]).astype(jnp.int32)
    share = unfolded.shape[1] // MODE
    starts = [sum(WIDTHS[:c]) for c in range(len(WIDTHS))]

    def columns(k, width):
        owner = ((position + k) & (MODE - 1)).astype(jnp.uint32)
        return lax.dynamic_slice_in_dim(unfolded, owner * share, width, axis=1)

    received, source = [], unfolded
    for start, width in zip(starts, WIDTHS):
        if start == 0:
            sent = {k: columns(k, width) for k in (2, 1, 3)}
        else:
            sent = dict(zip((2, 1, 3), column_slices(place, source, (2, 1, 3), start, width)))
        source, _ = lax.optimization_barrier((source, sent[2]))
        received.append([shift(sent[k], "mode", k) for k in range(1, MODE)])
    own = [column_slices(place, source, (0,), start, width)[0] for start, width in zip(starts, WIDTHS)]
    sums, wides = [None], []
    for c in range(len(WIDTHS)):
        wide, *sums = gram_lower(place, [own[c]] + received[c], sums[0], c == len(WIDTHS) - 1)
        wides.append(wide)
    sums = sum_everywhere(*sums)
    tri, basis = factorize(place, *sums, start_block, 1.0 / total_cols)
    basis_there = swap_cores(basis)
    factor = jnp.where(core_id == 1, basis, basis_there)
    triangle = unpack_triangle(place, tri, swap_cores(tri))
    landed = []
    for c, wide in enumerate(wides):
        parts = core_rows(place, basis, basis_there, wide)
        for k in (2, 1, 3, 0):
            got = shift(parts[k], "mode", k) if k else parts[0]
            landed.append((((position - k) & (MODE - 1)) * share + starts[c], got))
    core = jnp.zeros((factor.shape[1] // MODE, MODE * share), F32)
    core, triangle, factor, _ = lax.optimization_barrier((core, triangle, factor, parts[0]))
    for at, got in landed:
        core = lax.dynamic_update_slice_in_dim(core, got, at, axis=1)
    return (triangle, factor, core)


def solution(mesh):
    fine = Mesh(mesh.devices.reshape(4, 4, 8, 2), ("mode", "y", "z", "core"))
    rest = ("y", "z", "core")
    return jax.shard_map(
        per_device,
        mesh=fine,
        in_specs=(P("mode", rest), P()),
        out_specs=(P(), P(), P("mode", rest)),
        check_vma=False,
    )
```
